32 devices in a mesh: space: 16 (over z, y, x), src: 2 (over core).
Axes of the slice: x: 2, y: 2, z: 4, core: 2. Of those that a mesh axis runs over, the one named last changes fastest.
Arguments:
- rhs: float32 [12288, 1024], P('space', 'src'), may hold values from -18 to 18
- diag_blocks: bfloat16 [48, 256, 256], P('space', 'src'), may hold values from -0.5 to 5.5
- couple_blocks: bfloat16 [48, 2, 256, 256], P('space', None, 'src'), may hold values from -0.1875 to 0.1875
- halo_weight: bfloat16 [32, 256, 128], P('space', 'src'), may hold values from -0.25 to 0.25
- neighbours: int32 [48, 2], P('space'), may hold values from 0 to 2
- boundary: int32 [32, 128], P('space'), may hold values from 0 to 767
Outputs:
- solution: float32 [12288, 1024], P('space', 'src')
- misfit: float32 [1024], P('src')
The draws below stay inside these ranges and needn't reach their ends.
All inputs are finite; a program needn't handle non-finite values.
Results may differ from the reference program's by a relative error of at most 0.0032.
Values may be sent and summed in bfloat16 or wider, within the bound.
A program may use at most 64 MiB of HBM per device.

```python
import jax
import jax.numpy as jnp
from jax import lax

EDGE_AGG = 256
HALO = 128
NBR = 2
SWEEPS = 4
AGG_DEV = 3
SRC_DEV = 512
EDGES = 12288
AGGS = 48
SOURCES = 1024
N_SPACE = 16
N_SRC = 2


def draw_rhs(key, part):
    ramp = 1.0 + 2.0 * jnp.arange(EDGES, dtype=jnp.float32) / EDGES
    base = jnp.clip(jax.random.normal(key, (EDGES, SOURCES), jnp.float32), -6.0, 6.0)
    return base * ramp[:, None]


def draw_diag_blocks(key, part):
    first, second = jax.random.split(key)
    noise = jnp.clip(jax.random.normal(first, (AGGS, EDGE_AGG, EDGE_AGG), jnp.float32), -6.0, 6.0)
    noise = jnp.clip(noise / jnp.sqrt(jnp.float32(EDGE_AGG)), -0.5, 0.5)
    shifts = jax.random.uniform(second, (AGGS, EDGE_AGG, 1), jnp.float32, 3.0, 5.0)
    identity = jnp.eye(EDGE_AGG, dtype=jnp.float32)[None]
    return (noise + identity * shifts).astype(jnp.bfloat16)


def touch_ends(result, stream_key, smallest, largest):
    index_at = [jax.random.randint(jax.random.fold_in(stream_key, axis), (), 0, length) for axis, length in enumerate(result.shape)]
    main_axis = result.shape.index(max(result.shape))
    beside = index_at[:main_axis] + [(index_at[main_axis] + 1) % result.shape[main_axis]] + index_at[main_axis + 1:]
    return result.at[tuple(index_at)].set(smallest).at[tuple(beside)].set(largest)


def levels(rng, dims, cuts, low, top_value):
    loudness = 1.0
    for axis_at, blocks in cuts:
        heights = jax.random.uniform(jax.random.fold_in(jax.random.fold_in(rng, 6), axis_at), (blocks,), jnp.float32, low / len(cuts), top_value / len(cuts))
        loudness = loudness * jnp.repeat(jnp.exp(heights), dims[axis_at] // blocks).reshape((-1,) + (1,) * (len(dims) - 1 - axis_at))
    return loudness


def scatter_about(key, extent, spread, bound, pieces=(), kind=jnp.bfloat16):
    loudness = levels(key, extent, pieces, -0.22, 0.18) if pieces else 1.0
    result = jax.random.normal(key, extent, jnp.float32) * spread * loudness
    return jnp.minimum(jnp.maximum(result, -bound), bound).astype(kind)


def setup_inputs(seed: int = 0) -> dict:
    streams_of = jax.random.split(jax.random.key(seed), 7)
    rhs = draw_rhs(jax.random.fold_in(streams_of[6], 71), 0)
    diag_blocks = draw_diag_blocks(jax.random.fold_in(streams_of[6], 71), 0)
    couple_blocks = scatter_about(streams_of[2], (AGGS, NBR, EDGE_AGG, EDGE_AGG), (4 * EDGE_AGG) ** -0.5, 0.1875, ((0, 16), (2, 2)))
    halo_weight = scatter_about(streams_of[3], (2 * N_SPACE, EDGE_AGG, HALO), (4 * HALO) ** -0.5, 0.25, ((0, 16), (1, 2)))
    neighbours = touch_ends(jax.random.randint(streams_of[4], (AGGS, NBR), 0, AGG_DEV), jax.random.fold_in(streams_of[4], 1), 0, AGG_DEV - 1).astype(jnp.int32)
    boundary = touch_ends(jax.random.randint(streams_of[5], (2 * N_SPACE, HALO), 0, AGG_DEV * EDGE_AGG), jax.random.fold_in(streams_of[5], 1), 0, (AGG_DEV * EDGE_AGG) - 1).astype(jnp.int32)
    return {"rhs": rhs, "diag_blocks": diag_blocks, "couple_blocks": couple_blocks, "halo_weight": halo_weight, "neighbours": neighbours, "boundary": boundary}


centre = 4.0
half_width = 2.0

def pick_rows(block, index):
    return block[index]

def apply_operator(rounded, diag32, couple32, halo32, nbrs, bnds):
    values = rounded.astype(jnp.float32)
    high = lax.Precision.HIGHEST
    self_term = jnp.einsum('paij,pajs->pais', diag32, values, precision=high)
    beside = jax.vmap(pick_rows)(values, nbrs)
    cross_term = jnp.einsum('pakij,pakjs->pais', couple32, beside, precision=high)
    flat = values.reshape(N_SPACE, AGG_DEV * EDGE_AGG, values.shape[-1])
    picked = jax.vmap(pick_rows)(flat, bnds)
    empty = jnp.zeros_like(picked[:1, 0])
    from_below = jnp.concatenate([empty, picked[:-1, 1]], 0)
    from_above = jnp.concatenate([picked[1:, 0], empty], 0)
    lower = jnp.einsum('pih,phs->pis', halo32[:, 0], from_below, precision=high)
    upper = jnp.einsum('pih,phs->pis', halo32[:, 1], from_above, precision=high)
    total = self_term + cross_term
    total = total.at[:, 0].add(lower)
    total = total.at[:, AGG_DEV - 1].add(upper)
    return total

def reference(rhs, diag_blocks, couple_blocks, halo_weight, neighbours, boundary):
    diag32 = diag_blocks.astype(jnp.float32).reshape(N_SPACE, AGG_DEV, EDGE_AGG, EDGE_AGG)
    couple32 = couple_blocks.astype(jnp.float32).reshape(N_SPACE, AGG_DEV, NBR, EDGE_AGG, EDGE_AGG)
    halo32 = halo_weight.astype(jnp.float32).reshape(N_SPACE, 2, EDGE_AGG, HALO)
    nbrs = neighbours.reshape(N_SPACE, AGG_DEV, NBR).astype(jnp.int32)
    bnds = boundary.reshape(N_SPACE, 2, HALO).astype(jnp.int32)
    columns = rhs.reshape(EDGES, N_SRC, SRC_DEV).transpose(1, 0, 2)

    def smooth(right):
        shape4 = (N_SPACE, AGG_DEV, EDGE_AGG, SRC_DEV)
        residual = right.reshape(shape4)
        solution = jnp.zeros(shape4, jnp.float32)
        direction = residual / centre
        sigma = centre / half_width
        ratio = 1.0 / sigma
        for sweep in range(SWEEPS):
            solution = solution + direction
            image = apply_operator(direction.astype(jnp.bfloat16), diag32, couple32, halo32, nbrs, bnds)
            residual = residual - image
            if sweep + 1 < SWEEPS:
                ratio_new = 1.0 / (2.0 * sigma - ratio)
                direction = ratio_new * ratio * direction + 2.0 * ratio_new / half_width * residual
                ratio = ratio_new
        squares_res = lax.optimization_barrier(jnp.sum(residual * residual, axis=(0, 1, 2)))
        squares_rhs = lax.optimization_barrier(jnp.sum(right * right, axis=0))
        misfit = jnp.sqrt(squares_res / (squares_rhs + 1e-06))
        return (solution.reshape(EDGES, SRC_DEV), misfit)
    solution, misfit = lax.map(smooth, columns)
    return (solution.transpose(1, 0, 2).reshape(EDGES, SOURCES), misfit.reshape(SOURCES))
```

```python
import functools

import jax
import jax.numpy as jnp
from jax import lax
from jax.experimental import pallas as pl
from jax.experimental.pallas import tpu as pltpu
from jax.sharding import PartitionSpec as P

SWEEPS = 4
CHUNKS = 4
GROUP = 1
MESH = pl.DeviceIdType.MESH

centre = 4.0
half_width = 2.0


def sweep_weights():
    sigma = centre / half_width
    ratio = 1.0 / sigma
    weights = []
    for _ in range(SWEEPS - 1):
        ratio_new = 1.0 / (2.0 * sigma - ratio)
        weights.append((ratio_new * ratio, 2.0 * ratio_new / half_width))
        ratio = ratio_new
    return weights


def kernel(
    n_space, n_src,
    rhs_ref, diag_ref, couple_ref, halo_ref, nbr_hbm, bnd_ref,
    total, misfit_ref,
    res, dirn, rounded, weights, gmat, picks, spread, ahead, bounds, nbr_ref, outbox, inbox, red,
    rhs_sem, bnd_sem, nbr_sem, own_sem, op_send, op_recv, halo_send, halo_recv, sums_send, sums_recv, heard,
):
    me = lax.axis_index("space")
    core = lax.axis_index("src")
    aggs, size, depth = weights.shape
    edges, width = res.shape
    nbrs = couple_ref.shape[1]
    halo = bnd_ref.shape[1]
    part = size // n_src
    cols = width // CHUNKS
    bf16, f32 = jnp.bfloat16, jnp.float32

    def span(c, many=1):
        return pl.ds(c * cols, many * cols)

    def rows(a):
        return pl.ds(a * size, size)

    def dot(a, b):
        return jnp.dot(a, b, preferred_element_type=f32)

    rhs_loads = [
        pltpu.make_async_copy(rhs_ref.at[:, span(c)], res.at[:, span(c)], rhs_sem.at[c])
        for c in range(CHUNKS)
    ]
    bnd_load = pltpu.make_async_copy(bnd_ref, bounds, bnd_sem)
    bnd_load.start()
    for load in rhs_loads:
        load.start()
    mine = pl.ds(pl.multiple_of(core * part, part), part)
    pieces = [(diag_ref, weights.at[:, mine, pl.ds(0, size)])]
    for k in range(nbrs):
        pieces.append((couple_ref.at[:, k], weights.at[:, mine, pl.ds((k + 1) * size, size)]))
    pieces.append((halo_ref, gmat.at[:, mine]))
    own = [pltpu.make_async_copy(a, b, own_sem.at[i]) for i, (a, b) in enumerate(pieces)]
    nbr_load = pltpu.make_async_copy(nbr_hbm, nbr_ref, nbr_sem)
    nbr_load.start()
    for load in own:
        load.start()

    barrier = pltpu.get_barrier_semaphore()

    def greet(axis, to):
        pl.semaphore_signal(barrier, inc=1, device_id={axis: to}, device_id_type=MESH)

    def across(j):
        return me + (1 - 2 * (lax.div(me, 1 << j) % 2)) * (1 << j)

    hears = []
    if n_space & (n_space - 1) == 0:
        dims = n_space.bit_length() - 1
        for j in range(dims):
            greet("space", across(j))
        pl.when(me > 0)(lambda: greet("space", me - 1))
        pl.when(me < n_space - 1)(lambda: greet("space", me + 1))
        greeted = dims + (me > 0).astype(jnp.int32) + (me < n_space - 1).astype(jnp.int32)
        hears = list(range(1, dims))
    else:

        @pl.loop(1, n_space)
        def _(k):
            greet("space", lax.rem(me + k, n_space))

        greeted = n_space - 1
    for k in range(1, n_src):
        greet("src", lax.rem(core + k, n_src))

    last_heard = hears[-1] if hears else None

    def hear():
        j = hears.pop(0)
        if j > 1:
            pl.semaphore_wait(heard.at[j - 1], 1)
        pl.semaphore_signal(
            heard.at[j], inc=1, device_id={"space": across(j)}, device_id_type=MESH
        )

    bnd_load.wait()
    diagonal = lax.broadcasted_iota(jnp.int32, (halo, halo), 0) == lax.broadcasted_iota(
        jnp.int32, (halo, halo), 1
    )
    at = lax.broadcasted_iota(jnp.int32, (halo, edges), 1)
    for i, side in enumerate((1, 0)):
        listed = bounds[side : side + 1, :].astype(f32)
        column = jnp.sum(jnp.where(diagonal, listed, 0.0), axis=1, keepdims=True).astype(jnp.int32)
        picks[pl.ds(i * halo, halo), :] = (at == column).astype(f32).astype(bf16)

    @pl.when(me == 0)
    def _():
        inbox[:, :, 0] = jnp.zeros_like(inbox[:, :, 0])

    @pl.when(me == n_space - 1)
    def _():
        inbox[:, :, 1] = jnp.zeros_like(inbox[:, :, 1])

    def passed(s, c, side):
        to = lax.rem(me + 1, n_space) if side == 0 else lax.rem(me + n_space - 1, n_space)
        return pltpu.make_async_remote_copy(
            src_ref=outbox.at[s, c, side],
            dst_ref=inbox.at[s, c, side],
            send_sem=halo_send.at[s, c, side],
            recv_sem=halo_recv.at[s, c, side],
            device_id={"space": to},
            device_id_type=MESH,
        )

    sends = (me < n_space - 1, me > 0)
    takes = (me > 0, me < n_space - 1)

    def send(s, c):
        for side in range(2):
            pl.when(sends[side])(passed(s, c, side).start)

    def take(s, c):
        for side in range(2):
            pl.when(takes[side])(passed(s, c, side).wait_recv)

    moves = [
        pltpu.make_async_remote_copy(
            src_ref=a,
            dst_ref=b,
            send_sem=op_send.at[k - 1, i],
            recv_sem=op_recv.at[k - 1, i],
            device_id={"src": lax.rem(core + k, n_src)},
            device_id_type=MESH,
        )
        for k in range(1, n_src)
        for i, (a, b) in enumerate(pieces)
    ]

    for c in range(CHUNKS):
        rhs_loads[c].wait()
        right = res[:, span(c)]
        start = right * (1.0 / centre)
        dirn[:, span(c)] = start
        total[:, span(c)] = start
        first = start.astype(bf16)
        rounded[0, :, :, span(c)] = first.reshape(aggs, size, cols)
        outbox[0, c] = dot(picks[...], first).astype(bf16).reshape(2, halo, cols)
        if c == 0:
            pl.semaphore_wait(barrier, greeted + n_src - 1)
        send(0, c)
        if c == 0:
            for move in moves:
                move.start()
        red[me, 0:1, span(c)] = jnp.sum(right * right, axis=0, keepdims=True)

    if hears:
        hear()
    nbr_load.wait()
    for load in own:
        load.wait()
    for move in moves:
        move.wait()
    for side, a in ((0, 0), (1, aggs - 1)):
        spread[:, pl.ds(side * halo, halo)] = dot(picks[:, rows(a)], gmat[side]).astype(bf16)

    def local_part(c, now, later, keep, gain):
        wide = span(c, GROUP)
        ready = []
        for a in range(aggs):
            beside = [rounded[now, a, :, wide]]
            for k in range(nbrs):
                beside.append(rounded[now, nbr_ref[k, a], :, wide])
            left = res[rows(a), wide] - dot(weights[a], jnp.concatenate(beside, axis=0))
            res[rows(a), wide] = left
            if keep is not None:
                onward = keep * dirn[rows(a), wide] + gain * left
                dirn[rows(a), wide] = onward
                rounded[later, a, :, wide] = onward.astype(bf16)
                if 0 < a < aggs - 1:
                    total[rows(a), wide] += onward
        if keep is not None:
            ahead[:, wide] = dot(picks[...], rounded[later, :, :, wide].reshape(edges, GROUP * cols))

    def halo_part(s, c, later, gain):
        take(s, c)
        came = inbox[s, c].reshape(2 * halo, cols)
        onward = ahead[:, span(c)] - gain * dot(spread[...], came)
        outbox[s + 1, c] = onward.astype(bf16).reshape(2, halo, cols)
        send(s + 1, c)
        for side, a in ((0, 0), (1, aggs - 1)):
            pushed = dot(gmat[side], inbox[s, c, side])
            res[rows(a), span(c)] -= pushed
            step = dirn[rows(a), span(c)] - gain * pushed
            dirn[rows(a), span(c)] = step
            total[rows(a), span(c)] += step
            rounded[later, a, :, span(c)] = step.astype(bf16)

    steps = sweep_weights()
    for c in range(0, CHUNKS, GROUP):
        local_part(c, 0, 1, *steps[0])
    if hears:
        hear()
    for s in range(SWEEPS - 1):
        for c in range(CHUNKS):
            halo_part(s, c, (s + 1) % 2, steps[s][1])
            if (c + 1) % GROUP == 0:
                local_part(c + 1 - GROUP, (s + 1) % 2, s % 2, *(steps[s + 1] if s + 2 < SWEEPS else (None, None)))

    while hears:
        hear()
    for c in range(CHUNKS):
        take(SWEEPS - 1, c)
        squares = jnp.zeros((1, cols), f32)
        for a in range(aggs):
            left = res[rows(a), span(c)]
            for side, b in ((0, 0), (1, aggs - 1)):
                if a == b:
                    left = left - dot(gmat[side], inbox[SWEEPS - 1, c, side])
            squares = squares + jnp.sum(left * left, axis=0, keepdims=True)
        red[me, 1:2, span(c)] = squares
    if last_heard is not None:
        pl.semaphore_wait(heard.at[last_heard], 1)

    def share(k, carry):
        pltpu.make_async_remote_copy(
            src_ref=red.at[me],
            dst_ref=red.at[me],
            send_sem=sums_send,
            recv_sem=sums_recv,
            device_id={"space": lax.rem(me + k, n_space)},
            device_id_type=MESH,
        ).start()
        return carry

    lax.fori_loop(1, n_space, share, 0)
    for s in range(SWEEPS):
        for c in range(CHUNKS):
            for side in range(2):
                pl.when(sends[side])(passed(s, c, side).wait_send)
    others = red.at[pl.ds(0, n_space - 1)]
    pltpu.make_async_copy(others, others, sums_recv).wait()
    sums = jnp.sum(red[...], axis=0)
    misfit_ref[...] = jnp.sqrt(sums[1:2] / (sums[0:1] + 1e-06))
    pltpu.make_async_copy(others, others, sums_send).wait()


def store(total, misfit_ref, out, misfit_out, flat, sems):
    rows = total.shape[0] // CHUNKS
    copies = [
        pltpu.make_async_copy(total.at[pl.ds(c * rows, rows)], out.at[pl.ds(c * rows, rows)], sems.at[c])
        for c in range(CHUNKS)
    ]
    for copy in copies:
        copy.start()
    flat[...] = misfit_ref[0, :]
    copies.append(pltpu.make_async_copy(flat, misfit_out, sems.at[CHUNKS]))
    copies[-1].start()
    for copy in copies:
        copy.wait()


def local(n_space, n_src, rhs, diag_blocks, couple_blocks, halo_weight, neighbours, boundary):
    edges, width = rhs.shape
    aggs, part, size = diag_blocks.shape
    nbrs = couple_blocks.shape[1]
    halo = boundary.shape[1]
    cols = width // CHUNKS
    bf16, f32 = jnp.bfloat16, jnp.float32
    dma = pltpu.SemaphoreType.DMA
    outside = pl.BlockSpec(memory_space=pltpu.HBM)
    inside = pl.BlockSpec(memory_space=pltpu.VMEM)
    result, misfit = pl.pallas_call(
        functools.partial(kernel, n_space, n_src),
        out_shape=(
            pltpu.VMEM((edges, width), f32),
            pltpu.VMEM((1, width), f32),
        ),
        in_specs=[outside] * 6,
        out_specs=(inside, inside),
        scratch_shapes=[
            pltpu.VMEM((edges, width), f32),
            pltpu.VMEM((edges, width), f32),
            pltpu.VMEM((2, aggs, size, width), bf16),
            pltpu.VMEM((aggs, size, (nbrs + 1) * size), bf16),
            pltpu.VMEM((2, size, halo), bf16),
            pltpu.VMEM((2 * halo, edges), bf16),
            pltpu.VMEM((2 * halo, 2 * halo), bf16),
            pltpu.VMEM((2 * halo, width), f32),
            pltpu.VMEM((2, halo), jnp.int32),
            pltpu.SMEM((nbrs, aggs), jnp.int32),
            pltpu.VMEM((SWEEPS, CHUNKS, 2, halo, cols), bf16),
            pltpu.VMEM((SWEEPS, CHUNKS, 2, halo, cols), bf16),
            pltpu.VMEM((n_space, 2, width), f32),
            dma((CHUNKS,)),
            dma,
            dma,
            dma((nbrs + 2,)),
            dma((max(n_src - 1, 1), nbrs + 2)),
            dma((max(n_src - 1, 1), nbrs + 2)),
            dma((SWEEPS, CHUNKS, 2)),
            dma((SWEEPS, CHUNKS, 2)),
            dma,
            dma,
            pltpu.SemaphoreType.REGULAR((max(n_space.bit_length() - 1, 1),)),
        ],
        compiler_params=pltpu.CompilerParams(
            collective_id=0, has_side_effects=True, vmem_limit_bytes=(60 << 20) - edges * width * 4
        ),
    )(rhs, diag_blocks, couple_blocks, halo_weight, neighbours.T, boundary)
    return pl.pallas_call(
        store,
        out_shape=(
            jax.ShapeDtypeStruct((edges, width), f32),
            jax.ShapeDtypeStruct((width,), f32),
        ),
        in_specs=[inside, inside],
        out_specs=(outside, outside),
        scratch_shapes=[pltpu.VMEM((width,), f32), dma((CHUNKS + 1,))],
    )(
        pltpu.with_memory_space_constraint(result, pltpu.VMEM),
        pltpu.with_memory_space_constraint(misfit, pltpu.VMEM),
    )


def solution(mesh):
    placed = (
        P("space", "src"),
        P("space", "src", None),
        P("space", None, "src", None),
        P("space", "src", None),
        P("space", None),
        P("space", None),
    )
    body = functools.partial(local, mesh.shape["space"], mesh.shape["src"])
    return jax.shard_map(
        body, mesh=mesh, in_specs=placed, out_specs=(P("space", "src"), P("src")), check_vma=False
    )
```

```python
import functools

import jax
import jax.numpy as jnp
from jax import lax
from jax.experimental import pallas as pl
from jax.experimental.pallas import tpu as pltpu
from jax.sharding import PartitionSpec as P

SWEEPS = 4
CHUNKS = 4
GROUP = 1
MESH = pl.DeviceIdType.MESH

centre = 4.0
half_width = 2.0


def sweep_weights():
    sigma = centre / half_width
    ratio = 1.0 / sigma
    weights = []
    for _ in range(SWEEPS - 1):
        ratio_new = 1.0 / (2.0 * sigma - ratio)
        weights.append((ratio_new * ratio, 2.0 * ratio_new / half_width))
        ratio = ratio_new
    return weights


def kernel(
    n_space, n_src,
    rhs_ref, diag_ref, couple_ref, halo_ref, nbr_hbm, bnd_ref,
    total, misfit_ref,
    res, dirn, rounded, weights, gmat, picks, spread, ahead, bounds, nbr_ref, outbox, inbox, red,
    rhs_sem, bnd_sem, nbr_sem, own_sem, op_send, op_recv, halo_send, halo_recv, sums_send, sums_recv, heard,
):
    me = lax.axis_index("space")
    core = lax.axis_index("src")
    aggs, size, depth = weights.shape
    edges, width = res.shape
    nbrs = couple_ref.shape[1]
    halo = bnd_ref.shape[1]
    part = size // n_src
    cols = width // CHUNKS
    bf16, f32 = jnp.bfloat16, jnp.float32

    def span(c, many=1):
        return pl.ds(c * cols, many * cols)

    def rows(a):
        return pl.ds(a * size, size)

    def dot(a, b):
        return jnp.dot(a, b, preferred_element_type=f32)

    rhs_loads = [
        pltpu.make_async_copy(rhs_ref.at[:, span(c)], res.at[:, span(c)], rhs_sem.at[c])
        for c in range(CHUNKS)
    ]
    barrier = pltpu.get_barrier_semaphore()

    def greet(axis, to):
        pl.semaphore_signal(barrier, inc=1, device_id={axis: to}, device_id_type=MESH)

    def within(step):
        return ((me >= step, me - step), (me < n_space - step, me + step))

    def count(step):
        return sum(there.astype(jnp.int32) for there, _ in within(step))

    rhs_loads[0].start()
    bnd_load = pltpu.make_async_copy(bnd_ref, bounds, bnd_sem)
    bnd_load.start()
    for there, to in within(1):
        pl.when(there)(functools.partial(greet, "space", to))
    for k in range(1, n_src):
        greet("src", lax.rem(core + k, n_src))
    for load in rhs_loads[1:]:
        load.start()
    mine = pl.ds(pl.multiple_of(core * part, part), part)
    pieces = [(diag_ref, weights.at[:, mine, pl.ds(0, size)])]
    for k in range(nbrs):
        pieces.append((couple_ref.at[:, k], weights.at[:, mine, pl.ds((k + 1) * size, size)]))
    pieces.append((halo_ref, gmat.at[:, mine]))
    own = [pltpu.make_async_copy(a, b, own_sem.at[i]) for i, (a, b) in enumerate(pieces)]
    nbr_load = pltpu.make_async_copy(nbr_hbm, nbr_ref, nbr_sem)
    nbr_load.start()
    for load in own:
        load.start()

    levels = (n_space - 1).bit_length()
    told = []

    def tell():
        j = len(told)
        if j > levels:
            return
        if j > 0:
            known = count(1 << (j - 1))

            @pl.when(known > 0)
            def _():
                pl.semaphore_wait(heard.at[j - 1], known)

        if j < levels:
            for there, to in within(1 << j):

                @pl.when(there)
                def _():
                    pl.semaphore_signal(
                        heard.at[j], inc=1, device_id={"space": to}, device_id_type=MESH
                    )

        told.append(j)

    bnd_load.wait()
    diagonal = lax.broadcasted_iota(jnp.int32, (halo, halo), 0) == lax.broadcasted_iota(
        jnp.int32, (halo, halo), 1
    )
    at = lax.broadcasted_iota(jnp.int32, (halo, edges), 1)
    for i, side in enumerate((1, 0)):
        listed = bounds[side : side + 1, :].astype(f32)
        column = jnp.sum(jnp.where(diagonal, listed, 0.0), axis=1, keepdims=True).astype(jnp.int32)
        picks[pl.ds(i * halo, halo), :] = (at == column).astype(f32).astype(bf16)

    @pl.when(me == 0)
    def _():
        inbox[:, :, 0] = jnp.zeros_like(inbox[:, :, 0])

    @pl.when(me == n_space - 1)
    def _():
        inbox[:, :, 1] = jnp.zeros_like(inbox[:, :, 1])

    sides = []
    for k in range(2):
        side = lax.rem(me + 1 + k, 2)
        to = me + 1 - 2 * side
        sides.append((side, to, jnp.logical_and(to >= 0, to < n_space)))
    takes = (me > 0, me < n_space - 1)

    def send(s, c):
        for side, to, there in sides:
            pl.when(there)(
                pltpu.make_async_remote_copy(
                    src_ref=outbox.at[s, c, side],
                    dst_ref=inbox.at[s, c, side],
                    send_sem=halo_send,
                    recv_sem=halo_recv.at[s, c, side],
                    device_id={"space": to},
                    device_id_type=MESH,
                ).start
            )

    def take(s, c):
        for side in range(2):
            came = inbox.at[s, c, side]
            pl.when(takes[side])(pltpu.make_async_copy(came, came, halo_recv.at[s, c, side]).wait)

    moves = [
        pltpu.make_async_remote_copy(
            src_ref=a,
            dst_ref=b,
            send_sem=op_send.at[k - 1, i],
            recv_sem=op_recv.at[k - 1, i],
            device_id={"src": lax.rem(core + k, n_src)},
            device_id_type=MESH,
        )
        for k in range(1, n_src)
        for i, (a, b) in enumerate(pieces)
    ]

    for c in range(CHUNKS):
        rhs_loads[c].wait()
        right = res[:, span(c)]
        start = right * (1.0 / centre)
        dirn[:, span(c)] = start
        total[:, span(c)] = start
        first = start.astype(bf16)
        rounded[0, :, :, span(c)] = first.reshape(aggs, size, cols)
        outbox[0, c] = dot(picks[...], first).astype(bf16).reshape(2, halo, cols)
        if c == 0:
            pl.semaphore_wait(barrier, count(1) + n_src - 1)
        send(0, c)
        if c == 0:
            for move in moves:
                move.start()
        red[me, c : c + 1, :] = jnp.sum(right * right, axis=0, keepdims=True).astype(red.dtype)

    tell()
    nbr_load.wait()
    for load in own:
        load.wait()
    for move in moves:
        move.wait()
    for side, a in ((0, 0), (1, aggs - 1)):
        spread[:, pl.ds(side * halo, halo)] = dot(picks[:, rows(a)], gmat[side]).astype(bf16)

    def local_part(c, now, later, keep, gain):
        wide = span(c, GROUP)
        inner = []
        for a in range(aggs):
            beside = [rounded[now, a, :, wide]]
            for k in range(nbrs):
                beside.append(rounded[now, nbr_ref[k, a], :, wide])
            left = res[rows(a), wide] - dot(weights[a], jnp.concatenate(beside, axis=0))
            if keep is not None or not 0 < a < aggs - 1:
                res[rows(a), wide] = left
            else:
                inner.append(jnp.sum(left * left, axis=0, keepdims=True))
            if keep is not None:
                onward = keep * dirn[rows(a), wide] + gain * left
                dirn[rows(a), wide] = onward
                rounded[later, a, :, wide] = onward.astype(bf16)
                if 0 < a < aggs - 1:
                    total[rows(a), wide] += onward
        if keep is not None:
            ahead[:, wide] = dot(picks[...], rounded[later, :, :, wide].reshape(edges, GROUP * cols))
        else:
            ahead[0:1, wide] = sum(inner, jnp.zeros((1, GROUP * cols), f32))

    def halo_part(s, c, later, gain):
        take(s, c)
        came = inbox[s, c].reshape(2 * halo, cols)
        onward = ahead[:, span(c)] - gain * dot(spread[...], came)
        outbox[s + 1, c] = onward.astype(bf16).reshape(2, halo, cols)
        send(s + 1, c)
        for side, a in ((0, 0), (1, aggs - 1)):
            pushed = dot(gmat[side], inbox[s, c, side])
            res[rows(a), span(c)] -= pushed
            step = dirn[rows(a), span(c)] - gain * pushed
            dirn[rows(a), span(c)] = step
            total[rows(a), span(c)] += step
            rounded[later, a, :, span(c)] = step.astype(bf16)

    steps = sweep_weights()
    for c in range(0, CHUNKS, GROUP):
        local_part(c, 0, 1, *steps[0])
    tell()
    for s in range(SWEEPS - 1):
        for c in range(CHUNKS):
            halo_part(s, c, (s + 1) % 2, steps[s][1])
            if (c + 1) % GROUP == 0:
                local_part(c + 1 - GROUP, (s + 1) % 2, s % 2, *(steps[s + 1] if s + 2 < SWEEPS else (None, None)))
            if c % 2 == 1:
                tell()

    while len(told) <= levels:
        tell()
    for c in range(CHUNKS):
        take(SWEEPS - 1, c)
        squares = ahead[0:1, span(c)]
        for side, a in ((0, 0), (1, aggs - 1)):
            left = res[rows(a), span(c)] - dot(gmat[side], inbox[SWEEPS - 1, c, side])
            squares = squares + jnp.sum(left * left, axis=0, keepdims=True)
        red[me, CHUNKS + c : CHUNKS + c + 1, :] = squares.astype(red.dtype)

    def share(k, carry):
        pltpu.make_async_remote_copy(
            src_ref=red.at[me],
            dst_ref=red.at[me],
            send_sem=sums_send,
            recv_sem=sums_recv,
            device_id={"space": k + (k >= me).astype(jnp.int32)},
            device_id_type=MESH,
        ).start()
        return carry

    lax.fori_loop(0, n_space - 1, share, 0)
    for _, _, there in sides:
        sent = outbox.at[:, :, 0]
        pl.when(there)(pltpu.make_async_copy(sent, sent, halo_send).wait)
    others = red.at[pl.ds(0, n_space - 1)]
    pltpu.make_async_copy(others, others, sums_recv).wait()
    sums = jnp.sum(red[...].astype(f32), axis=0)
    misfit_ref[...] = jnp.sqrt(sums[CHUNKS:] / (sums[:CHUNKS] + 1e-06))
    pltpu.make_async_copy(others, others, sums_send).wait()


def store(total, misfit_ref, out, misfit_out, flat, sems):
    rows = total.shape[0] // CHUNKS
    copies = [
        pltpu.make_async_copy(total.at[pl.ds(c * rows, rows)], out.at[pl.ds(c * rows, rows)], sems.at[c])
        for c in range(CHUNKS)
    ]
    for copy in copies:
        copy.start()
    chunks, cols = misfit_ref.shape
    for c in range(chunks):
        flat[pl.ds(c * cols, cols)] = misfit_ref[c, :]
    copies.append(pltpu.make_async_copy(flat, misfit_out, sems.at[CHUNKS]))
    copies[-1].start()
    for copy in copies:
        copy.wait()


def local(n_space, n_src, rhs, diag_blocks, couple_blocks, halo_weight, neighbours, boundary):
    edges, width = rhs.shape
    aggs, part, size = diag_blocks.shape
    nbrs = couple_blocks.shape[1]
    halo = boundary.shape[1]
    cols = width // CHUNKS
    bf16, f32 = jnp.bfloat16, jnp.float32
    dma = pltpu.SemaphoreType.DMA
    outside = pl.BlockSpec(memory_space=pltpu.HBM)
    inside = pl.BlockSpec(memory_space=pltpu.VMEM)
    result, misfit = pl.pallas_call(
        functools.partial(kernel, n_space, n_src),
        out_shape=(
            pltpu.VMEM((edges, width), f32),
            pltpu.VMEM((CHUNKS, cols), f32),
        ),
        in_specs=[outside] * 6,
        out_specs=(inside, inside),
        scratch_shapes=[
            pltpu.VMEM((edges, width), f32),
            pltpu.VMEM((edges, width), f32),
            pltpu.VMEM((2, aggs, size, width), bf16),
            pltpu.VMEM((aggs, size, (nbrs + 1) * size), bf16),
            pltpu.VMEM((2, size, halo), bf16),
            pltpu.VMEM((2 * halo, edges), bf16),
            pltpu.VMEM((2 * halo, 2 * halo), bf16),
            pltpu.VMEM((2 * halo, width), f32),
            pltpu.VMEM((2, halo), jnp.int32),
            pltpu.SMEM((nbrs, aggs), jnp.int32),
            pltpu.VMEM((SWEEPS, CHUNKS, 2, halo, cols), bf16),
            pltpu.VMEM((SWEEPS, CHUNKS, 2, halo, cols), bf16),
            pltpu.VMEM((n_space, 2 * CHUNKS, cols), f32),
            dma((CHUNKS,)),
            dma,
            dma,
            dma((nbrs + 2,)),
            dma((max(n_src - 1, 1), nbrs + 2)),
            dma((max(n_src - 1, 1), nbrs + 2)),
            dma,
            dma((SWEEPS, CHUNKS, 2)),
            dma,
            dma,
            pltpu.SemaphoreType.REGULAR((max((n_space - 1).bit_length(), 1),)),
        ],
        compiler_params=pltpu.CompilerParams(
            collective_id=0, has_side_effects=True, vmem_limit_bytes=(60 << 20) - edges * width * 4
        ),
    )(rhs, diag_blocks, couple_blocks, halo_weight, neighbours.T, boundary)
    return pl.pallas_call(
        store,
        out_shape=(
            jax.ShapeDtypeStruct((edges, width), f32),
            jax.ShapeDtypeStruct((width,), f32),
        ),
        in_specs=[inside, inside],
        out_specs=(outside, outside),
        scratch_shapes=[pltpu.VMEM((width,), f32), dma((CHUNKS + 1,))],
    )(
        pltpu.with_memory_space_constraint(result, pltpu.VMEM),
        pltpu.with_memory_space_constraint(misfit, pltpu.VMEM),
    )


def solution(mesh):
    placed = (
        P("space", "src"),
        P("space", "src", None),
        P("space", None, "src", None),
        P("space", "src", None),
        P("space", None),
        P("space", None),
    )
    body = functools.partial(local, mesh.shape["space"], mesh.shape["src"])
    return jax.shard_map(
        body, mesh=mesh, in_specs=placed, out_specs=(P("space", "src"), P("src")), check_vma=False
    )
```

```python
import functools

import jax
import jax.numpy as jnp
from jax import lax
from jax.experimental import pallas as pl
from jax.experimental.pallas import tpu as pltpu
from jax.sharding import PartitionSpec as P

SWEEPS = 4
CHUNKS = 4
GROUP = 2
FIRST = 2
MESH = pl.DeviceIdType.MESH

centre = 4.0
half_width = 2.0


def sweep_weights():
    sigma = centre / half_width
    ratio = 1.0 / sigma
    weights = []
    for _ in range(SWEEPS - 1):
        ratio_new = 1.0 / (2.0 * sigma - ratio)
        weights.append((ratio_new * ratio, 2.0 * ratio_new / half_width))
        ratio = ratio_new
    return weights


def kernel(
    n_space, n_src,
    rhs_ref, diag_ref, couple_ref, halo_ref, nbr_hbm, bnd_ref,
    total, misfit_ref,
    res, dirn, rounded, weights, gmat, picks, spread, ahead, bounds, nbr_ref, outbox, inbox, red,
    rhs_sem, bnd_sem, nbr_sem, own_sem, op_send, op_recv, halo_send, halo_recv, sums_send, sums_recv, heard,
):
    me = lax.axis_index("space")
    core = lax.axis_index("src")
    aggs, size, depth = weights.shape
    edges, width = res.shape
    nbrs = couple_ref.shape[1]
    halo = bnd_ref.shape[1]
    part = size // n_src
    cols = width // CHUNKS
    bf16, f32 = jnp.bfloat16, jnp.float32

    def span(c, many=1):
        return pl.ds(c * cols, many * cols)

    def rows(a):
        return pl.ds(a * size, size)

    def dot(a, b):
        return jnp.dot(a, b, preferred_element_type=f32)

    rhs_loads = [
        pltpu.make_async_copy(rhs_ref.at[:, span(c)], res.at[:, span(c)], rhs_sem.at[c])
        for c in range(CHUNKS)
    ]
    barrier = pltpu.get_barrier_semaphore()

    def greet(axis, to):
        pl.semaphore_signal(barrier, inc=1, device_id={axis: to}, device_id_type=MESH)

    def within(step):
        return ((me >= step, me - step), (me < n_space - step, me + step))

    def count(step):
        return sum(there.astype(jnp.int32) for there, _ in within(step))

    rhs_loads[0].start()
    bnd_load = pltpu.make_async_copy(bnd_ref, bounds, bnd_sem)
    bnd_load.start()
    for there, to in within(1):
        pl.when(there)(functools.partial(greet, "space", to))
    for k in range(1, n_src):
        greet("src", lax.rem(core + k, n_src))
    for load in rhs_loads[1:]:
        load.start()
    mine = pl.ds(pl.multiple_of(core * part, part), part)
    pieces = [(diag_ref, weights.at[:, mine, pl.ds(0, size)])]
    for k in range(nbrs):
        pieces.append((couple_ref.at[:, k], weights.at[:, mine, pl.ds((k + 1) * size, size)]))
    pieces.append((halo_ref, gmat.at[:, mine]))
    own = [pltpu.make_async_copy(a, b, own_sem.at[i]) for i, (a, b) in enumerate(pieces)]
    nbr_load = pltpu.make_async_copy(nbr_hbm, nbr_ref, nbr_sem)
    nbr_load.start()
    for load in own:
        load.start()

    levels = (n_space - 1).bit_length()
    told = []

    def tell():
        j = len(told)
        if j > levels:
            return
        if j > 0:
            known = count(1 << (j - 1))

            @pl.when(known > 0)
            def _():
                pl.semaphore_wait(heard.at[j - 1], known)

        if j < levels:
            for there, to in within(1 << j):

                @pl.when(there)
                def _():
                    pl.semaphore_signal(
                        heard.at[j], inc=1, device_id={"space": to}, device_id_type=MESH
                    )

        told.append(j)

    bnd_load.wait()
    diagonal = lax.broadcasted_iota(jnp.int32, (halo, halo), 0) == lax.broadcasted_iota(
        jnp.int32, (halo, halo), 1
    )
    at = lax.broadcasted_iota(jnp.int32, (halo, edges), 1)
    for i, side in enumerate((1, 0)):
        listed = bounds[side : side + 1, :].astype(f32)
        column = jnp.sum(jnp.where(diagonal, listed, 0.0), axis=1, keepdims=True).astype(jnp.int32)
        picks[pl.ds(i * halo, halo), :] = (at == column).astype(f32).astype(bf16)

    @pl.when(me == 0)
    def _():
        inbox[:, :, 0] = jnp.zeros_like(inbox[:, :, 0])

    @pl.when(me == n_space - 1)
    def _():
        inbox[:, :, 1] = jnp.zeros_like(inbox[:, :, 1])

    sides = []
    for k in range(2):
        side = lax.rem(me + 1 + k, 2)
        to = me + 1 - 2 * side
        sides.append((side, to, jnp.logical_and(to >= 0, to < n_space)))
    takes = (me > 0, me < n_space - 1)

    even = lax.rem(core, 2) == 0

    def send(s, c, when=True):
        for side, to, there in sides:
            pl.when(jnp.logical_and(there, when))(
                pltpu.make_async_remote_copy(
                    src_ref=outbox.at[s, c, side],
                    dst_ref=inbox.at[s, c, side],
                    send_sem=halo_send,
                    recv_sem=halo_recv.at[s, c, side],
                    device_id={"space": to},
                    device_id_type=MESH,
                ).start
            )

    def take(s, c):
        for side in range(2):
            came = inbox.at[s, c, side]
            pl.when(takes[side])(pltpu.make_async_copy(came, came, halo_recv.at[s, c, side]).wait)

    moves = [
        pltpu.make_async_remote_copy(
            src_ref=a,
            dst_ref=b,
            send_sem=op_send.at[k - 1, i],
            recv_sem=op_recv.at[k - 1, i],
            device_id={"src": lax.rem(core + k, n_src)},
            device_id_type=MESH,
        )
        for k in range(1, n_src)
        for i, (a, b) in enumerate(pieces)
    ]

    for c in range(CHUNKS):
        rhs_loads[c].wait()
        right = res[:, span(c)]
        start = right * (1.0 / centre)
        dirn[:, span(c)] = start
        total[:, span(c)] = start
        first = start.astype(bf16)
        rounded[0, :, :, span(c)] = first.reshape(aggs, size, cols)
        outbox[0, c] = dot(picks[...], first).astype(bf16).reshape(2, halo, cols)
        if c == 0:
            pl.semaphore_wait(barrier, count(1) + n_src - 1)
        send(0, c)
        if c == 0:
            for move in moves:
                move.start()
        red[me, c : c + 1, :] = jnp.sum(right * right, axis=0, keepdims=True).astype(red.dtype)

    tell()
    nbr_load.wait()
    for load in own:
        load.wait()
    for move in moves:
        move.wait()
    for side, a in ((0, 0), (1, aggs - 1)):
        spread[:, pl.ds(side * halo, halo)] = dot(picks[:, rows(a)], gmat[side]).astype(bf16)

    def local_part(c, many, now, later, keep, gain):
        wide = span(c, many)
        inner = []
        for a in range(aggs):
            beside = [rounded[now, a, :, wide]]
            for k in range(nbrs):
                beside.append(rounded[now, nbr_ref[k, a], :, wide])
            left = res[rows(a), wide] - dot(weights[a], jnp.concatenate(beside, axis=0))
            if keep is not None or not 0 < a < aggs - 1:
                res[rows(a), wide] = left
            else:
                inner.append(jnp.sum(left * left, axis=0, keepdims=True))
            if keep is not None:
                onward = keep * dirn[rows(a), wide] + gain * left
                dirn[rows(a), wide] = onward
                rounded[later, a, :, wide] = onward.astype(bf16)
                if 0 < a < aggs - 1:
                    total[rows(a), wide] += onward
        if keep is not None:
            ahead[:, wide] = dot(picks[...], rounded[later, :, :, wide].reshape(edges, many * cols))
        else:
            ahead[0:1, wide] = sum(inner, jnp.zeros((1, many * cols), f32))

    def halo_part(s, c, later, gain):
        take(s, c)
        came = inbox[s, c].reshape(2 * halo, cols)
        onward = ahead[:, span(c)] - gain * dot(spread[...], came)
        outbox[s + 1, c] = onward.astype(bf16).reshape(2, halo, cols)
        send(s + 1, c, even)
        for side, a in ((0, 0), (1, aggs - 1)):
            pushed = dot(gmat[side], inbox[s, c, side])
            res[rows(a), span(c)] -= pushed
            step = dirn[rows(a), span(c)] - gain * pushed
            dirn[rows(a), span(c)] = step
            total[rows(a), span(c)] += step
            rounded[later, a, :, span(c)] = step.astype(bf16)

    steps = sweep_weights()
    for c in range(0, CHUNKS, FIRST):
        local_part(c, FIRST, 0, 1, *steps[0])
    tell()
    for s in range(SWEEPS - 1):
        for c in range(CHUNKS):
            halo_part(s, c, (s + 1) % 2, steps[s][1])
            if (c + 1) % GROUP == 0:
                local_part(c + 1 - GROUP, GROUP, (s + 1) % 2, s % 2, *(steps[s + 1] if s + 2 < SWEEPS else (None, None)))
            if (c + 1) % GROUP == 0:
                for d in range(c + 1 - GROUP, c + 1):
                    send(s + 1, d, jnp.logical_not(even))
            if c % 2 == 1:
                tell()

    while len(told) <= levels:
        tell()
    for c in range(CHUNKS):
        take(SWEEPS - 1, c)
        squares = ahead[0:1, span(c)]
        for side, a in ((0, 0), (1, aggs - 1)):
            left = res[rows(a), span(c)] - dot(gmat[side], inbox[SWEEPS - 1, c, side])
            squares = squares + jnp.sum(left * left, axis=0, keepdims=True)
        red[me, CHUNKS + c : CHUNKS + c + 1, :] = squares.astype(red.dtype)

    def share(k, carry):
        pltpu.make_async_remote_copy(
            src_ref=red.at[me],
            dst_ref=red.at[me],
            send_sem=sums_send,
            recv_sem=sums_recv,
            device_id={"space": k + (k >= me).astype(jnp.int32)},
            device_id_type=MESH,
        ).start()
        return carry

    lax.fori_loop(0, n_space - 1, share, 0)
    for _, _, there in sides:
        sent = outbox.at[:, :, 0]
        pl.when(there)(pltpu.make_async_copy(sent, sent, halo_send).wait)
    others = red.at[pl.ds(0, n_space - 1)]
    pltpu.make_async_copy(others, others, sums_recv).wait()
    sums = jnp.sum(red[...].astype(f32), axis=0)
    misfit_ref[...] = jnp.sqrt(sums[CHUNKS:] / (sums[:CHUNKS] + 1e-06))
    pltpu.make_async_copy(others, others, sums_send).wait()


def store(total, misfit_ref, out, misfit_out, flat, sems):
    rows = total.shape[0] // CHUNKS
    copies = [
        pltpu.make_async_copy(total.at[pl.ds(c * rows, rows)], out.at[pl.ds(c * rows, rows)], sems.at[c])
        for c in range(CHUNKS)
    ]
    for copy in copies:
        copy.start()
    chunks, cols = misfit_ref.shape
    for c in range(chunks):
        flat[pl.ds(c * cols, cols)] = misfit_ref[c, :]
    copies.append(pltpu.make_async_copy(flat, misfit_out, sems.at[CHUNKS]))
    copies[-1].start()
    for copy in copies:
        copy.wait()


def local(n_space, n_src, rhs, diag_blocks, couple_blocks, halo_weight, neighbours, boundary):
    edges, width = rhs.shape
    aggs, part, size = diag_blocks.shape
    nbrs = couple_blocks.shape[1]
    halo = boundary.shape[1]
    cols = width // CHUNKS
    bf16, f32 = jnp.bfloat16, jnp.float32
    dma = pltpu.SemaphoreType.DMA
    outside = pl.BlockSpec(memory_space=pltpu.HBM)
    inside = pl.BlockSpec(memory_space=pltpu.VMEM)
    result, misfit = pl.pallas_call(
        functools.partial(kernel, n_space, n_src),
        out_shape=(
            pltpu.VMEM((edges, width), f32),
            pltpu.VMEM((CHUNKS, cols), f32),
        ),
        in_specs=[outside] * 6,
        out_specs=(inside, inside),
        scratch_shapes=[
            pltpu.VMEM((edges, width), f32),
            pltpu.VMEM((edges, width), f32),
            pltpu.VMEM((2, aggs, size, width), bf16),
            pltpu.VMEM((aggs, size, (nbrs + 1) * size), bf16),
            pltpu.VMEM((2, size, halo), bf16),
            pltpu.VMEM((2 * halo, edges), bf16),
            pltpu.VMEM((2 * halo, 2 * halo), bf16),
            pltpu.VMEM((2 * halo, width), f32),
            pltpu.VMEM((2, halo), jnp.int32),
            pltpu.SMEM((nbrs, aggs), jnp.int32),
            pltpu.VMEM((SWEEPS, CHUNKS, 2, halo, cols), bf16),
            pltpu.VMEM((SWEEPS, CHUNKS, 2, halo, cols), bf16),
            pltpu.VMEM((n_space, 2 * CHUNKS, cols), f32),
            dma((CHUNKS,)),
            dma,
            dma,
            dma((nbrs + 2,)),
            dma((max(n_src - 1, 1), nbrs + 2)),
            dma((max(n_src - 1, 1), nbrs + 2)),
            dma,
            dma((SWEEPS, CHUNKS, 2)),
            dma,
            dma,
            pltpu.SemaphoreType.REGULAR((max((n_space - 1).bit_length(), 1),)),
        ],
        compiler_params=pltpu.CompilerParams(
            collective_id=0, has_side_effects=True, vmem_limit_bytes=(60 << 20) - edges * width * 4
        ),
    )(rhs, diag_blocks, couple_blocks, halo_weight, neighbours.T, boundary)
    return pl.pallas_call(
        store,
        out_shape=(
            jax.ShapeDtypeStruct((edges, width), f32),
            jax.ShapeDtypeStruct((width,), f32),
        ),
        in_specs=[inside, inside],
        out_specs=(outside, outside),
        scratch_shapes=[pltpu.VMEM((width,), f32), dma((CHUNKS + 1,))],
    )(
        pltpu.with_memory_space_constraint(result, pltpu.VMEM),
        pltpu.with_memory_space_constraint(misfit, pltpu.VMEM),
    )


def solution(mesh):
    placed = (
        P("space", "src"),
        P("space", "src", None),
        P("space", None, "src", None),
        P("space", "src", None),
        P("space", None),
        P("space", None),
    )
    body = functools.partial(local, mesh.shape["space"], mesh.shape["src"])
    return jax.shard_map(
        body, mesh=mesh, in_specs=placed, out_specs=(P("space", "src"), P("src")), check_vma=False
    )
```

```python
import functools

import jax
import jax.numpy as jnp
from jax import lax
from jax.experimental import pallas as pl
from jax.experimental.pallas import tpu as pltpu
from jax.sharding import PartitionSpec as P

SWEEPS = 4
CHUNKS = 4
GROUP = 2
FIRST = 2
MESH = pl.DeviceIdType.MESH

centre = 4.0
half_width = 2.0


def sweep_weights():
    sigma = centre / half_width
    ratio = 1.0 / sigma
    weights = []
    for _ in range(SWEEPS - 1):
        ratio_new = 1.0 / (2.0 * sigma - ratio)
        weights.append((ratio_new * ratio, 2.0 * ratio_new / half_width))
        ratio = ratio_new
    return weights


def kernel(
    n_space, n_src,
    rhs_ref, diag_ref, couple_ref, halo_ref, nbr_hbm, bnd_ref,
    total, misfit_ref,
    res, dirn, rounded, weights, gmat, picks, spread, ahead, bounds, nbr_ref, outbox, inbox, red,
    rhs_sem, bnd_sem, nbr_sem, own_sem, op_send, op_recv, halo_send, halo_recv, sums_send, sums_recv, heard,
):
    me = lax.axis_index("space")
    core = lax.axis_index("src")
    aggs, size, depth = weights.shape
    edges, width = res.shape
    nbrs = couple_ref.shape[1]
    halo = bnd_ref.shape[1]
    part = size // n_src
    cols = width // CHUNKS
    bf16, f32 = jnp.bfloat16, jnp.float32

    def span(c, many=1):
        return pl.ds(c * cols, many * cols)

    def rows(a):
        return pl.ds(a * size, size)

    def dot(a, b):
        return jnp.dot(a, b, preferred_element_type=f32)

    rhs_loads = [
        pltpu.make_async_copy(rhs_ref.at[:, span(c)], res.at[:, span(c)], rhs_sem.at[c])
        for c in range(CHUNKS)
    ]
    barrier = pltpu.get_barrier_semaphore()

    def greet(axis, to):
        pl.semaphore_signal(barrier, inc=1, device_id={axis: to}, device_id_type=MESH)

    def within(step):
        return ((me >= step, me - step), (me < n_space - step, me + step))

    def count(step):
        return sum(there.astype(jnp.int32) for there, _ in within(step))

    rhs_loads[0].start()
    bnd_load = pltpu.make_async_copy(bnd_ref, bounds, bnd_sem)
    bnd_load.start()
    for there, to in within(1):
        pl.when(there)(functools.partial(greet, "space", to))
    for k in range(1, n_src):
        greet("src", lax.rem(core + k, n_src))
    for load in rhs_loads[1:]:
        load.start()
    mine = pl.ds(pl.multiple_of(core * part, part), part)
    pieces = [(diag_ref, weights.at[:, mine, pl.ds(0, size)])]
    for k in range(nbrs):
        pieces.append((couple_ref.at[:, k], weights.at[:, mine, pl.ds((k + 1) * size, size)]))
    pieces.append((halo_ref, gmat.at[:, mine]))
    own = [pltpu.make_async_copy(a, b, own_sem.at[i]) for i, (a, b) in enumerate(pieces)]
    nbr_load = pltpu.make_async_copy(nbr_hbm, nbr_ref, nbr_sem)
    nbr_load.start()
    for load in own:
        load.start()

    levels = (n_space - 1).bit_length()
    told = []

    def tell():
        j = len(told)
        if j > levels:
            return
        if j > 0:
            known = count(1 << (j - 1))

            @pl.when(known > 0)
            def _():
                pl.semaphore_wait(heard.at[j - 1], known)

        if j < levels:
            for there, to in within(1 << j):

                @pl.when(there)
                def _():
                    pl.semaphore_signal(
                        heard.at[j], inc=1, device_id={"space": to}, device_id_type=MESH
                    )

        told.append(j)

    bnd_load.wait()
    diagonal = lax.broadcasted_iota(jnp.int32, (halo, halo), 0) == lax.broadcasted_iota(
        jnp.int32, (halo, halo), 1
    )
    at = lax.broadcasted_iota(jnp.int32, (halo, edges), 1)
    for i, side in enumerate((1, 0)):
        listed = bounds[side : side + 1, :].astype(f32)
        column = jnp.sum(jnp.where(diagonal, listed, 0.0), axis=1, keepdims=True).astype(jnp.int32)
        picks[pl.ds(i * halo, halo), :] = (at == column).astype(f32).astype(bf16)

    @pl.when(me == 0)
    def _():
        inbox[:, :, 0] = jnp.zeros_like(inbox[:, :, 0])

    @pl.when(me == n_space - 1)
    def _():
        inbox[:, :, 1] = jnp.zeros_like(inbox[:, :, 1])

    sides = []
    for k in range(2):
        side = lax.rem(me + 1 + k, 2)
        to = me + 1 - 2 * side
        sides.append((side, to, jnp.logical_and(to >= 0, to < n_space)))
    takes = (me > 0, me < n_space - 1)

    even = lax.rem(core, 2) == 0

    def send(s, c, when=True):
        for side, to, there in sides:
            pl.when(jnp.logical_and(there, when))(
                pltpu.make_async_remote_copy(
                    src_ref=outbox.at[s, c, side],
                    dst_ref=inbox.at[s, c, side],
                    send_sem=halo_send,
                    recv_sem=halo_recv.at[s, c, side],
                    device_id={"space": to},
                    device_id_type=MESH,
                ).start
            )

    def take(s, c):
        for side in range(2):
            came = inbox.at[s, c, side]
            pl.when(takes[side])(pltpu.make_async_copy(came, came, halo_recv.at[s, c, side]).wait)

    moves = [
        pltpu.make_async_remote_copy(
            src_ref=a,
            dst_ref=b,
            send_sem=op_send.at[k - 1, i],
            recv_sem=op_recv.at[k - 1, i],
            device_id={"src": lax.rem(core + k, n_src)},
            device_id_type=MESH,
        )
        for k in range(1, n_src)
        for i, (a, b) in enumerate(pieces)
    ]

    for c in range(CHUNKS):
        rhs_loads[c].wait()
        right = res[:, span(c)]
        start = right * (1.0 / centre)
        dirn[:, span(c)] = start
        total[:, span(c)] = start
        first = start.astype(bf16)
        rounded[0, :, :, span(c)] = first.reshape(aggs, size, cols)
        outbox[0, c] = dot(picks[...], first).astype(bf16).reshape(2, halo, cols)
        if c == 0:
            pl.semaphore_wait(barrier, count(1) + n_src - 1)
        send(0, c)
        if c == 0:
            for move in moves:
                move.start()
        red[me, c : c + 1, :] = jnp.sum(right * right, axis=0, keepdims=True).astype(red.dtype)

    tell()
    nbr_load.wait()
    for load in own:
        load.wait()
    for move in moves:
        move.wait()
    for side, a in ((0, 0), (1, aggs - 1)):
        spread[:, pl.ds(side * halo, halo)] = dot(picks[:, rows(a)], gmat[side]).astype(bf16)

    def local_part(c, many, now, later, keep, gain):
        wide = span(c, many)
        inner = []
        for a in range(aggs):
            beside = [rounded[now, a, :, wide]]
            for k in range(nbrs):
                beside.append(rounded[now, nbr_ref[k, a], :, wide])
            left = res[rows(a), wide] - dot(weights[a], jnp.concatenate(beside, axis=0))
            if keep is not None or not 0 < a < aggs - 1:
                res[rows(a), wide] = left
            else:
                inner.append(jnp.sum(left * left, axis=0, keepdims=True))
            if keep is not None:
                onward = keep * dirn[rows(a), wide] + gain * left
                dirn[rows(a), wide] = onward
                rounded[later, a, :, wide] = onward.astype(bf16)
                if 0 < a < aggs - 1:
                    total[rows(a), wide] += onward
        if keep is not None:
            ahead[:, wide] = dot(picks[...], rounded[later, :, :, wide].reshape(edges, many * cols))
        else:
            ahead[0:1, wide] = sum(inner, jnp.zeros((1, many * cols), f32))

    def halo_part(s, c, later, gain):
        take(s, c)
        came = inbox[s, c].reshape(2 * halo, cols)
        onward = ahead[:, span(c)] - gain * dot(spread[...], came)
        outbox[s + 1, c] = onward.astype(bf16).reshape(2, halo, cols)
        send(s + 1, c, True if s + 2 == SWEEPS else even)
        for side, a in ((0, 0), (1, aggs - 1)):
            pushed = dot(gmat[side], inbox[s, c, side])
            res[rows(a), span(c)] -= pushed
            step = dirn[rows(a), span(c)] - gain * pushed
            dirn[rows(a), span(c)] = step
            total[rows(a), span(c)] += step
            rounded[later, a, :, span(c)] = step.astype(bf16)

    steps = sweep_weights()
    for c in range(0, CHUNKS, FIRST):
        local_part(c, FIRST, 0, 1, *steps[0])
    tell()
    for s in range(SWEEPS - 1):
        for c in range(CHUNKS):
            halo_part(s, c, (s + 1) % 2, steps[s][1])
            if (c + 1) % GROUP == 0:
                local_part(c + 1 - GROUP, GROUP, (s + 1) % 2, s % 2, *(steps[s + 1] if s + 2 < SWEEPS else (None, None)))
            if (c + 1) % GROUP == 0:
                for d in range(c + 1 - GROUP, c + 1 if s + 2 < SWEEPS else 0):
                    send(s + 1, d, jnp.logical_not(even))
            if c % 2 == 1:
                tell()

    while len(told) <= levels:
        tell()
    for c in range(CHUNKS):
        take(SWEEPS - 1, c)
        squares = ahead[0:1, span(c)]
        for side, a in ((0, 0), (1, aggs - 1)):
            left = res[rows(a), span(c)] - dot(gmat[side], inbox[SWEEPS - 1, c, side])
            squares = squares + jnp.sum(left * left, axis=0, keepdims=True)
        red[me, CHUNKS + c : CHUNKS + c + 1, :] = squares.astype(red.dtype)

    def share(k, carry):
        pltpu.make_async_remote_copy(
            src_ref=red.at[me],
            dst_ref=red.at[me],
            send_sem=sums_send,
            recv_sem=sums_recv,
            device_id={"space": k + (k >= me).astype(jnp.int32)},
            device_id_type=MESH,
        ).start()
        return carry

    lax.fori_loop(0, n_space - 1, share, 0)
    for _, _, there in sides:
        sent = outbox.at[:, :, 0]
        pl.when(there)(pltpu.make_async_copy(sent, sent, halo_send).wait)
    others = red.at[pl.ds(0, n_space - 1)]
    pltpu.make_async_copy(others, others, sums_recv).wait()
    sums = jnp.sum(red[...].astype(f32), axis=0)
    misfit_ref[...] = jnp.sqrt(sums[CHUNKS:] / (sums[:CHUNKS] + 1e-06))
    pltpu.make_async_copy(others, others, sums_send).wait()


def store(total, misfit_ref, out, misfit_out, flat, sems):
    rows = total.shape[0] // CHUNKS
    copies = [
        pltpu.make_async_copy(total.at[pl.ds(c * rows, rows)], out.at[pl.ds(c * rows, rows)], sems.at[c])
        for c in range(CHUNKS)
    ]
    for copy in copies:
        copy.start()
    chunks, cols = misfit_ref.shape
    for c in range(chunks):
        flat[pl.ds(c * cols, cols)] = misfit_ref[c, :]
    copies.append(pltpu.make_async_copy(flat, misfit_out, sems.at[CHUNKS]))
    copies[-1].start()
    for copy in copies:
        copy.wait()


def local(n_space, n_src, rhs, diag_blocks, couple_blocks, halo_weight, neighbours, boundary):
    edges, width = rhs.shape
    aggs, part, size = diag_blocks.shape
    nbrs = couple_blocks.shape[1]
    halo = boundary.shape[1]
    cols = width // CHUNKS
    bf16, f32 = jnp.bfloat16, jnp.float32
    dma = pltpu.SemaphoreType.DMA
    outside = pl.BlockSpec(memory_space=pltpu.HBM)
    inside = pl.BlockSpec(memory_space=pltpu.VMEM)
    result, misfit = pl.pallas_call(
        functools.partial(kernel, n_space, n_src),
        out_shape=(
            pltpu.VMEM((edges, width), f32),
            pltpu.VMEM((CHUNKS, cols), f32),
        ),
        in_specs=[outside] * 6,
        out_specs=(inside, inside),
        scratch_shapes=[
            pltpu.VMEM((edges, width), f32),
            pltpu.VMEM((edges, width), f32),
            pltpu.VMEM((2, aggs, size, width), bf16),
            pltpu.VMEM((aggs, size, (nbrs + 1) * size), bf16),
            pltpu.VMEM((2, size, halo), bf16),
            pltpu.VMEM((2 * halo, edges), bf16),
            pltpu.VMEM((2 * halo, 2 * halo), bf16),
            pltpu.VMEM((2 * halo, width), f32),
            pltpu.VMEM((2, halo), jnp.int32),
            pltpu.SMEM((nbrs, aggs), jnp.int32),
            pltpu.VMEM((SWEEPS, CHUNKS, 2, halo, cols), bf16),
            pltpu.VMEM((SWEEPS, CHUNKS, 2, halo, cols), bf16),
            pltpu.VMEM((n_space, 2 * CHUNKS, cols), f32),
            dma((CHUNKS,)),
            dma,
            dma,
            dma((nbrs + 2,)),
            dma((max(n_src - 1, 1), nbrs + 2)),
            dma((max(n_src - 1, 1), nbrs + 2)),
            dma,
            dma((SWEEPS, CHUNKS, 2)),
            dma,
            dma,
            pltpu.SemaphoreType.REGULAR((max((n_space - 1).bit_length(), 1),)),
        ],
        compiler_params=pltpu.CompilerParams(
            collective_id=0, has_side_effects=True, vmem_limit_bytes=(60 << 20) - edges * width * 4
        ),
    )(rhs, diag_blocks, couple_blocks, halo_weight, neighbours.T, boundary)
    return pl.pallas_call(
        store,
        out_shape=(
            jax.ShapeDtypeStruct((edges, width), f32),
            jax.ShapeDtypeStruct((width,), f32),
        ),
        in_specs=[inside, inside],
        out_specs=(outside, outside),
        scratch_shapes=[pltpu.VMEM((width,), f32), dma((CHUNKS + 1,))],
    )(
        pltpu.with_memory_space_constraint(result, pltpu.VMEM),
        pltpu.with_memory_space_constraint(misfit, pltpu.VMEM),
    )


def solution(mesh):
    placed = (
        P("space", "src"),
        P("space", "src", None),
        P("space", None, "src", None),
        P("space", "src", None),
        P("space", None),
        P("space", None),
    )
    body = functools.partial(local, mesh.shape["space"], mesh.shape["src"])
    return jax.shard_map(
        body, mesh=mesh, in_specs=placed, out_specs=(P("space", "src"), P("src")), check_vma=False
    )
```

```python
import functools

import jax
import jax.numpy as jnp
from jax import lax
from jax.experimental import pallas as pl
from jax.experimental.pallas import tpu as pltpu
from jax.sharding import PartitionSpec as P

SWEEPS = 4
CHUNKS = 4
GROUP = 2
FIRST = 2
MESH = pl.DeviceIdType.MESH

centre = 4.0
half_width = 2.0


def sweep_weights():
    sigma = centre / half_width
    ratio = 1.0 / sigma
    weights = []
    for _ in range(SWEEPS - 1):
        ratio_new = 1.0 / (2.0 * sigma - ratio)
        weights.append((ratio_new * ratio, 2.0 * ratio_new / half_width))
        ratio = ratio_new
    return weights


def kernel(
    n_space, n_src,
    rhs_ref, diag_ref, couple_ref, halo_ref, nbr_hbm, bnd_ref,
    total, misfit_ref,
    res, dirn, rounded, weights, gmat, picks, spread, ahead, bounds, nbr_ref, outbox, inbox, red,
    rhs_sem, bnd_sem, nbr_sem, own_sem, op_send, op_recv, halo_send, halo_recv, sums_send, sums_recv, heard,
):
    me = lax.axis_index("space")
    core = lax.axis_index("src")
    aggs, size, depth = weights.shape
    edges, width = res.shape
    nbrs = couple_ref.shape[1]
    halo = bnd_ref.shape[1]
    part = size // n_src
    cols = width // CHUNKS
    bf16, f32 = jnp.bfloat16, jnp.float32

    def span(c, many=1):
        return pl.ds(c * cols, many * cols)

    def rows(a):
        return pl.ds(a * size, size)

    def dot(a, b):
        return jnp.dot(a, b, preferred_element_type=f32)

    rhs_loads = [
        pltpu.make_async_copy(rhs_ref.at[:, span(c)], res.at[:, span(c)], rhs_sem.at[c])
        for c in range(CHUNKS)
    ]
    barrier = pltpu.get_barrier_semaphore()

    def greet(axis, to):
        pl.semaphore_signal(barrier, inc=1, device_id={axis: to}, device_id_type=MESH)

    def within(step):
        return ((me >= step, me - step), (me < n_space - step, me + step))

    def count(step):
        return sum(there.astype(jnp.int32) for there, _ in within(step))

    rhs_loads[0].start()
    bnd_load = pltpu.make_async_copy(bnd_ref, bounds, bnd_sem)
    bnd_load.start()
    for there, to in within(1):
        pl.when(there)(functools.partial(greet, "space", to))
    for k in range(1, n_src):
        greet("src", lax.rem(core + k, n_src))
    for load in rhs_loads[1:]:
        load.start()
    mine = pl.ds(pl.multiple_of(core * part, part), part)
    pieces = [(diag_ref, weights.at[:, mine, pl.ds(0, size)])]
    for k in range(nbrs):
        pieces.append((couple_ref.at[:, k], weights.at[:, mine, pl.ds((k + 1) * size, size)]))
    pieces.append((halo_ref, gmat.at[:, mine]))
    own = [pltpu.make_async_copy(a, b, own_sem.at[i]) for i, (a, b) in enumerate(pieces)]
    nbr_load = pltpu.make_async_copy(nbr_hbm, nbr_ref, nbr_sem)
    nbr_load.start()
    for load in own:
        load.start()

    levels = (n_space - 1).bit_length()
    told = []

    def tell():
        j = len(told)
        if j > levels:
            return
        if j > 0:
            known = count(1 << (j - 1))

            @pl.when(known > 0)
            def _():
                pl.semaphore_wait(heard.at[j - 1], known)

        if j < levels:
            for there, to in within(1 << j):

                @pl.when(there)
                def _():
                    pl.semaphore_signal(
                        heard.at[j], inc=1, device_id={"space": to}, device_id_type=MESH
                    )

        told.append(j)

    bnd_load.wait()
    diagonal = lax.broadcasted_iota(jnp.int32, (halo, halo), 0) == lax.broadcasted_iota(
        jnp.int32, (halo, halo), 1
    )
    at = lax.broadcasted_iota(jnp.int32, (halo, edges), 1)
    for i, side in enumerate((1, 0)):
        listed = bounds[side : side + 1, :].astype(f32)
        column = jnp.sum(jnp.where(diagonal, listed, 0.0), axis=1, keepdims=True).astype(jnp.int32)
        picks[pl.ds(i * halo, halo), :] = (at == column).astype(f32).astype(bf16)

    @pl.when(me == 0)
    def _():
        inbox[:, :, 0] = jnp.zeros_like(inbox[:, :, 0])

    @pl.when(me == n_space - 1)
    def _():
        inbox[:, :, 1] = jnp.zeros_like(inbox[:, :, 1])

    sides = []
    for k in range(2):
        side = lax.rem(me + 1 + k, 2)
        to = me + 1 - 2 * side
        sides.append((side, to, jnp.logical_and(to >= 0, to < n_space)))
    takes = (me > 0, me < n_space - 1)

    even = lax.rem(core, 2) == 0

    def send(s, c, when=True):
        for side, to, there in sides:
            pl.when(jnp.logical_and(there, when))(
                pltpu.make_async_remote_copy(
                    src_ref=outbox.at[s, c, side],
                    dst_ref=inbox.at[s, c, side],
                    send_sem=halo_send,
                    recv_sem=halo_recv.at[s, c, side],
                    device_id={"space": to},
                    device_id_type=MESH,
                ).start
            )

    def take(s, c):
        for side in range(2):
            came = inbox.at[s, c, side]
            pl.when(takes[side])(pltpu.make_async_copy(came, came, halo_recv.at[s, c, side]).wait)

    moves = [
        pltpu.make_async_remote_copy(
            src_ref=a,
            dst_ref=b,
            send_sem=op_send.at[k - 1, i],
            recv_sem=op_recv.at[k - 1, i],
            device_id={"src": lax.rem(core + k, n_src)},
            device_id_type=MESH,
        )
        for k in range(1, n_src)
        for i, (a, b) in enumerate(pieces)
    ]

    for c in range(CHUNKS):
        rhs_loads[c].wait()
        right = res[:, span(c)]
        start = right * (1.0 / centre)
        dirn[:, span(c)] = start
        total[:, span(c)] = start
        first = start.astype(bf16)
        rounded[0, :, :, span(c)] = first.reshape(aggs, size, cols)
        outbox[0, c] = dot(picks[...], first).astype(bf16).reshape(2, halo, cols)
        if c == 0:
            pl.semaphore_wait(barrier, count(1) + n_src - 1)
        send(0, c)
        if c == 0:
            for move in moves:
                move.start()
        red[me, c : c + 1, :] = jnp.sum(right * right, axis=0, keepdims=True).astype(red.dtype)

    tell()
    nbr_load.wait()
    for load in own:
        load.wait()
    for move in moves:
        move.wait()
    for side, a in ((0, 0), (1, aggs - 1)):
        spread[:, pl.ds(side * halo, halo)] = dot(picks[:, rows(a)], gmat[side]).astype(bf16)

    def local_part(c, many, now, later, keep, gain):
        wide = span(c, many)
        inner = []
        for a in range(aggs):
            beside = [rounded[now, a, :, wide]]
            for k in range(nbrs):
                beside.append(rounded[now, nbr_ref[k, a], :, wide])
            left = res[rows(a), wide] - dot(weights[a], jnp.concatenate(beside, axis=0))
            if keep is not None or not 0 < a < aggs - 1:
                res[rows(a), wide] = left
            else:
                inner.append(jnp.sum(left * left, axis=0, keepdims=True))
            if keep is not None:
                onward = keep * dirn[rows(a), wide] + gain * left
                dirn[rows(a), wide] = onward
                rounded[later, a, :, wide] = onward.astype(bf16)
                if 0 < a < aggs - 1:
                    total[rows(a), wide] += onward
        if keep is not None:
            ahead[:, wide] = dot(picks[...], rounded[later, :, :, wide].reshape(edges, many * cols))
        else:
            ahead[0:1, wide] = sum(inner, jnp.zeros((1, many * cols), f32))

    def halo_part(s, c, later, gain):
        take(s, c)
        came = inbox[s, c].reshape(2 * halo, cols)
        onward = ahead[:, span(c)] - gain * dot(spread[...], came)
        outbox[s + 1, c] = onward.astype(bf16).reshape(2, halo, cols)
        send(s + 1, c, True if s + 2 == SWEEPS else even)
        for side, a in ((0, 0), (1, aggs - 1)):
            pushed = dot(gmat[side], inbox[s, c, side])
            res[rows(a), span(c)] -= pushed
            step = dirn[rows(a), span(c)] - gain * pushed
            dirn[rows(a), span(c)] = step
            total[rows(a), span(c)] += step
            rounded[later, a, :, span(c)] = step.astype(bf16)

    steps = sweep_weights()
    for c in range(0, CHUNKS, FIRST):
        local_part(c, FIRST, 0, 1, *steps[0])
    tell()
    for s in range(SWEEPS - 1):
        for c in range(CHUNKS):
            halo_part(s, c, (s + 1) % 2, steps[s][1])
            if (c + 1) % GROUP == 0:
                local_part(c + 1 - GROUP, GROUP, (s + 1) % 2, s % 2, *(steps[s + 1] if s + 2 < SWEEPS else (None, None)))
            if (c + 1) % GROUP == 0 and s + 2 < SWEEPS:

                @pl.when(jnp.logical_not(even))
                def _():
                    for d in range(c + 1 - GROUP, c + 1):
                        send(s + 1, d)

            if c % 2 == 1:
                tell()

    while len(told) <= levels:
        tell()
    for c in range(CHUNKS):
        take(SWEEPS - 1, c)
        squares = ahead[0:1, span(c)]
        for side, a in ((0, 0), (1, aggs - 1)):
            left = res[rows(a), span(c)] - dot(gmat[side], inbox[SWEEPS - 1, c, side])
            squares = squares + jnp.sum(left * left, axis=0, keepdims=True)
        red[me, CHUNKS + c : CHUNKS + c + 1, :] = squares.astype(red.dtype)

    def share(k, carry):
        pltpu.make_async_remote_copy(
            src_ref=red.at[me],
            dst_ref=red.at[me],
            send_sem=sums_send,
            recv_sem=sums_recv,
            device_id={"space": k + (k >= me).astype(jnp.int32)},
            device_id_type=MESH,
        ).start()
        return carry

    lax.fori_loop(0, n_space - 1, share, 0)
    for _, _, there in sides:
        sent = outbox.at[:, :, 0]
        pl.when(there)(pltpu.make_async_copy(sent, sent, halo_send).wait)
    others = red.at[pl.ds(0, n_space - 1)]
    pltpu.make_async_copy(others, others, sums_recv).wait()
    sums = jnp.sum(red[...].astype(f32), axis=0)
    misfit_ref[...] = jnp.sqrt(sums[CHUNKS:] / (sums[:CHUNKS] + 1e-06))
    pltpu.make_async_copy(others, others, sums_send).wait()


def store(total, misfit_ref, out, misfit_out, flat, sems):
    rows = total.shape[0] // CHUNKS
    copies = [
        pltpu.make_async_copy(total.at[pl.ds(c * rows, rows)], out.at[pl.ds(c * rows, rows)], sems.at[c])
        for c in range(CHUNKS)
    ]
    for copy in copies:
        copy.start()
    chunks, cols = misfit_ref.shape
    for c in range(chunks):
        flat[pl.ds(c * cols, cols)] = misfit_ref[c, :]
    copies.append(pltpu.make_async_copy(flat, misfit_out, sems.at[CHUNKS]))
    copies[-1].start()
    for copy in copies:
        copy.wait()


def local(n_space, n_src, rhs, diag_blocks, couple_blocks, halo_weight, neighbours, boundary):
    edges, width = rhs.shape
    aggs, part, size = diag_blocks.shape
    nbrs = couple_blocks.shape[1]
    halo = boundary.shape[1]
    cols = width // CHUNKS
    bf16, f32 = jnp.bfloat16, jnp.float32
    dma = pltpu.SemaphoreType.DMA
    outside = pl.BlockSpec(memory_space=pltpu.HBM)
    inside = pl.BlockSpec(memory_space=pltpu.VMEM)
    result, misfit = pl.pallas_call(
        functools.partial(kernel, n_space, n_src),
        out_shape=(
            pltpu.VMEM((edges, width), f32),
            pltpu.VMEM((CHUNKS, cols), f32),
        ),
        in_specs=[outside] * 6,
        out_specs=(inside, inside),
        scratch_shapes=[
            pltpu.VMEM((edges, width), f32),
            pltpu.VMEM((edges, width), f32),
            pltpu.VMEM((2, aggs, size, width), bf16),
            pltpu.VMEM((aggs, size, (nbrs + 1) * size), bf16),
            pltpu.VMEM((2, size, halo), bf16),
            pltpu.VMEM((2 * halo, edges), bf16),
            pltpu.VMEM((2 * halo, 2 * halo), bf16),
            pltpu.VMEM((2 * halo, width), f32),
            pltpu.VMEM((2, halo), jnp.int32),
            pltpu.SMEM((nbrs, aggs), jnp.int32),
            pltpu.VMEM((SWEEPS, CHUNKS, 2, halo, cols), bf16),
            pltpu.VMEM((SWEEPS, CHUNKS, 2, halo, cols), bf16),
            pltpu.VMEM((n_space, 2 * CHUNKS, cols), f32),
            dma((CHUNKS,)),
            dma,
            dma,
            dma((nbrs + 2,)),
            dma((max(n_src - 1, 1), nbrs + 2)),
            dma((max(n_src - 1, 1), nbrs + 2)),
            dma,
            dma((SWEEPS, CHUNKS, 2)),
            dma,
            dma,
            pltpu.SemaphoreType.REGULAR((max((n_space - 1).bit_length(), 1),)),
        ],
        compiler_params=pltpu.CompilerParams(
            collective_id=0, has_side_effects=True, vmem_limit_bytes=(60 << 20) - edges * width * 4
        ),
    )(rhs, diag_blocks, couple_blocks, halo_weight, neighbours.T, boundary)
    return pl.pallas_call(
        store,
        out_shape=(
            jax.ShapeDtypeStruct((edges, width), f32),
            jax.ShapeDtypeStruct((width,), f32),
        ),
        in_specs=[inside, inside],
        out_specs=(outside, outside),
        scratch_shapes=[pltpu.VMEM((width,), f32), dma((CHUNKS + 1,))],
    )(
        pltpu.with_memory_space_constraint(result, pltpu.VMEM),
        pltpu.with_memory_space_constraint(misfit, pltpu.VMEM),
    )


def solution(mesh):
    placed = (
        P("space", "src"),
        P("space", "src", None),
        P("space", None, "src", None),
        P("space", "src", None),
        P("space", None),
        P("space", None),
    )
    body = functools.partial(local, mesh.shape["space"], mesh.shape["src"])
    return jax.shard_map(
        body, mesh=mesh, in_specs=placed, out_specs=(P("space", "src"), P("src")), check_vma=False
    )
```
